32 devices in a mesh: pa: 4 (over y, core), pb: 8 (over z, x).
Axes of the slice: x: 2, y: 2, z: 4, core: 2. Of those that a mesh axis runs over, the one named last changes fastest.
Arguments:
- excitons: bfloat16 [2, 512, 1024], P(None, 'pa', 'pb'), may hold values from -6 to 6
- screened: bfloat16 [16384, 16384], P('pa', 'pb'), may hold values from -0.25 to 0.25
- phi_val: bfloat16 [16384, 512], P('pa'), may hold values from -0.25 to 0.25
- phi_con: bfloat16 [16384, 1024], P('pb'), may hold values from -0.1875 to 0.1875
Outputs:
- kernel_out: bfloat16 [2, 512, 1024], P(None, 'pa', 'pb')
The draws below stay inside these ranges and needn't reach their ends.
All inputs are finite; a program needn't handle non-finite values.
Results may differ from the reference program's by a relative error of at most 0.0057.
Values may be sent and summed in bfloat16 or wider, within the bound.
No kernel may reach another device: no remote copies, remote signals or barrier semaphores. Data moves between devices by JAX's collectives and lax.ppermute only.
A program may use at most 192 MiB of HBM per device.

```python
import math
import jax
import jax.numpy as jnp
from jax import lax

NV = 512
NC = 1024
NPTS = 16384
NEX = 2


def level_of(stream_key, shape, split, smallest, top_value):
    def one(position, blocks):
        draws = jax.random.uniform(jax.random.fold_in(jax.random.fold_in(stream_key, 6), position), (blocks,), jnp.float32, smallest / len(split), top_value / len(split))
        return jnp.repeat(jnp.exp(draws), shape[position] // blocks).reshape((-1,) + (1,) * (len(shape) - position - 1))

    level = one(*split[0])
    for cut in split[1:]:
        level = level * one(*cut)
    return level


def scatter_about(rng, extent, deviation, bound, pieces=(), held_as=jnp.bfloat16):
    result = jax.random.normal(rng, extent, jnp.float32) * deviation
    if len(pieces) > 0:
        result = level_of(rng, extent, pieces, -0.22, 0.18) * result
    return jnp.clip(result, min=-bound, max=bound).astype(held_as)


def setup_inputs(seed: int = 0) -> dict:
    seeds = jax.random.split(jax.random.key(seed), 5)
    excitons = scatter_about(seeds[0], (NEX, NV, NC), 1.0, 6.0, ((1, 4), (2, 8)))
    screened = scatter_about(seeds[1], (NPTS, NPTS), ((NV * NC) ** 0.5 / NPTS), 0.25, ((0, 4), (1, 8)))
    phi_val = scatter_about(seeds[2], (NPTS, NV), NV ** -0.5, 0.25, ((0, 4),))
    phi_con = scatter_about(seeds[3], (NPTS, NC), NC ** -0.5, 0.1875, ((0, 8),))
    return dict(excitons=excitons, screened=screened, phi_val=phi_val, phi_con=phi_con)


def reference(excitons, screened, phi_val, phi_con):
    high = lax.Precision.HIGHEST
    val_f = phi_val.astype(jnp.float32)
    con_f = phi_con.astype(jnp.float32)
    wide_f = screened.astype(jnp.float32)
    block = math.gcd(NPTS, 1024)
    count = NPTS // block

    def one(single):
        half_exp = jnp.dot(single.astype(jnp.float32), con_f.T, precision=high).astype(jnp.bfloat16)
        half_exp = lax.optimization_barrier(half_exp).astype(jnp.float32)

        def step(total, index):
            start = (index * block).astype(jnp.int32)
            val_rows = lax.dynamic_slice_in_dim(val_f, start, block, 0)
            wide_rows = lax.dynamic_slice_in_dim(wide_f, start, block, 0)
            expanded = jnp.dot(val_rows, half_exp, precision=high)
            weighted = (wide_rows * expanded).astype(jnp.bfloat16)
            weighted = lax.optimization_barrier(weighted).astype(jnp.float32)
            return total + jnp.dot(val_rows.T, weighted, precision=high), None

        start_total = jnp.zeros((NV, NPTS), jnp.float32)
        back_val, _ = lax.scan(step, start_total, jnp.arange(count, dtype=jnp.int32))
        return jnp.dot(back_val, con_f, precision=high).astype(jnp.bfloat16)

    return lax.map(one, excitons)
```

```python
import functools

import jax
import jax.numpy as jnp
from jax import lax
from jax.experimental import pallas as pl
from jax.experimental.pallas import tpu as pltpu
from jax.sharding import PartitionSpec as P

TILE_P = 512


def xor_pairs(size, mask):
    return [(i, i ^ mask) for i in range(size)]


def swap_blocks(array, me, order, width):
    rows, columns = array.shape
    count = columns // width
    blocks = array.reshape(rows, count, width)
    bit = 1
    while bit < count:
        pairs = blocks.reshape(rows, count // (2 * bit), 2, bit, width)
        swapped = jnp.flip(pairs, axis=2)
        blocks = jnp.where((me & bit) != 0, swapped, pairs).reshape(rows, count, width)
        bit *= 2
    return jnp.stack([blocks[:, j] for j in order], axis=1).reshape(rows, columns)


def fused_kernel(exc_ref, con_ref, val_ref, scr_ref, keep_ref, send_ref, half, acc):
    step = pl.program_id(0)

    @pl.when(step == 0)
    def _():
        half[...] = lax.dot_general(
            exc_ref[...], con_ref[...], (((1,), (1,)), ((), ())),
            preferred_element_type=jnp.float32,
        ).astype(half.dtype)
        acc[...] = jnp.zeros_like(acc)

    val = val_ref[...]
    expanded = jnp.dot(val, half[...], preferred_element_type=jnp.float32)
    weighted = (scr_ref[...].astype(jnp.float32) * expanded).astype(jnp.bfloat16)
    acc[...] += lax.dot_general(
        val, weighted, (((0,), (0,)), ((), ())), preferred_element_type=jnp.float32
    )

    @pl.when(step == pl.num_programs(0) - 1)
    def _():
        back = acc[...].astype(jnp.bfloat16)
        terms = jnp.dot(back, con_ref[...], preferred_element_type=jnp.float32)
        rows = keep_ref.shape[0]
        keep_ref[...] = terms[:rows].astype(keep_ref.dtype)
        send_ref[...] = terms[rows:].astype(send_ref.dtype)


def apply_block(exc, con, val, screened):
    nv, nc = exc.shape
    np_, nq = screened.shape
    tile = min(TILE_P, np_)
    whole = lambda shape: pl.BlockSpec(shape, lambda i: (0, 0), pipeline_mode=pl.Buffered(1))
    flops = 2 * nv * nc * nq * 2 + 4 * np_ * nq * nv
    return pl.pallas_call(
        fused_kernel,
        out_shape=(
            jax.ShapeDtypeStruct((nv // 2, nc), jnp.bfloat16),
            jax.ShapeDtypeStruct((nv // 2, nc), jnp.bfloat16),
        ),
        grid=(np_ // tile,),
        in_specs=[
            whole((nv, nc)),
            whole((nq, nc)),
            pl.BlockSpec((tile, nv), lambda i: (i, 0)),
            pl.BlockSpec((tile, nq), lambda i: (i, 0)),
        ],
        out_specs=(whole((nv // 2, nc)), whole((nv // 2, nc))),
        scratch_shapes=[
            pltpu.VMEM((nv, nq), jnp.bfloat16),
            pltpu.VMEM((nv, nq), jnp.float32),
        ],
        cost_estimate=pl.CostEstimate(
            flops=flops, transcendentals=0, bytes_accessed=2 * (np_ * nq + np_ * nv + nq * nc)
        ),
    )(exc, con, val, screened)


def gather(block, axis, size, low, dim):
    high = size // low
    if high > 1:
        block = jnp.concatenate(
            [block] + [lax.ppermute(block, axis, xor_pairs(size, k * low)) for k in range(1, high)], dim
        )
    if low > 1:
        block = jnp.concatenate(
            [block] + [lax.ppermute(block, axis, xor_pairs(size, k)) for k in range(1, low)], dim
        )
    return block


def order_of(size, low):
    high = size // low
    return [h * low + l for l in range(low) for h in range(high)]


def pieces(array, count, dim):
    width = array.shape[dim] // count
    return [lax.slice_in_dim(array, k * width, (k + 1) * width, axis=dim) for k in range(count)]


def scatter_stage(parts, axis, size, stride):
    total = parts[0].astype(jnp.float32)
    for k in range(1, len(parts)):
        total = total + lax.ppermute(
            parts[k].astype(jnp.bfloat16), axis, xor_pairs(size, k * stride)
        ).astype(jnp.float32)
    return total


def solution(mesh):
    na, nb = mesh.shape["pa"], mesh.shape["pb"]
    low_a = 2
    low_b = max(nb // 4, 1)
    order_a, order_b = order_of(na, low_a), order_of(nb, low_b)

    def local(excitons, screened, phi_val, phi_con):
        me_a, me_b = lax.axis_index("pa"), lax.axis_index("pb")
        vb, cb = excitons.shape[1:]
        val = swap_blocks(phi_val, me_a, order_a, vb)
        con = swap_blocks(phi_con, me_b, order_b, cb)
        results = []
        for e in range(excitons.shape[0]):
            rows = gather(excitons[e], "pb", nb, low_b, 1)
            exc = gather(rows, "pa", na, low_a, 0)
            keep, send = apply_block(exc, con, val, screened)
            total = scatter_stage([keep, send], "pa", na, 1)
            total = scatter_stage(pieces(total, na // low_a, 0), "pa", na, low_a)
            total = scatter_stage(pieces(total, low_b, 1), "pb", nb, 1)
            total = scatter_stage(pieces(total, nb // low_b, 1), "pb", nb, low_b)
            results.append(total.astype(jnp.bfloat16))
        return jnp.stack(results)

    placed = (P(None, "pa", "pb"), P("pa", "pb"), P("pa", None), P("pb", None))
    return jax.shard_map(
        local, mesh=mesh, in_specs=placed, out_specs=P(None, "pa", "pb"), check_vma=False
    )
```

```python
import functools

import jax
import jax.numpy as jnp
from jax import lax
from jax.experimental import pallas as pl
from jax.experimental.pallas import tpu as pltpu
from jax.sharding import PartitionSpec as P

TILE_P = 512
LANES = 128


def xor_pairs(size, mask):
    return [(i, i ^ mask) for i in range(size)]


def xor_columns(value, me, width):
    columns = value.shape[1]
    bit = 1
    while bit * width < columns:
        half = bit * width
        flipped = jnp.concatenate(
            [value[:, (k ^ 1) * half : ((k ^ 1) + 1) * half] for k in range(columns // half)], axis=1
        )
        value = jnp.where(lax.broadcast((me & bit) != 0, value.shape), flipped, value)
        bit *= 2
    return value


def fused_kernel(order_a, order_b, rows_keep, me_ref, *refs):
    count = len(order_a)
    exc_refs = refs[:count]
    con_ref, val_ref, scr_ref = refs[count : count + 3]
    keep_refs = refs[count + 3 : count + 3 + rows_keep]
    send_ref = refs[count + 3 + rows_keep]
    exc, half, acc, terms = refs[count + 4 + rows_keep :]
    vb, nc = exc_refs[0].shape
    cb = nc // len(order_b)
    step = pl.program_id(0)
    me_a, me_b = me_ref[0], me_ref[1]
    aligned = cb % LANES == 0

    def row(rel):
        return pl.ds(pl.multiple_of((me_a ^ rel) * vb, vb), vb)

    def column(rel):
        return pl.ds(pl.multiple_of((me_b ^ rel) * cb, cb), cb)

    @pl.when(step == 0)
    def _():
        for i, rel_a in enumerate(order_a):
            if aligned:
                for j, rel_b in enumerate(order_b):
                    exc[row(rel_a), column(rel_b)] = exc_refs[i][:, j * cb : (j + 1) * cb]
            else:
                place = {rel_b: j for j, rel_b in enumerate(order_b)}
                value = exc_refs[i][...]
                value = jnp.concatenate(
                    [value[:, place[k] * cb : (place[k] + 1) * cb] for k in range(len(order_b))], axis=1
                )
                exc[row(rel_a), :] = xor_columns(value, me_b, cb)
        half[...] = lax.dot_general(
            exc[...], con_ref[...], (((1,), (1,)), ((), ())), preferred_element_type=jnp.float32
        ).astype(half.dtype)
        acc[...] = jnp.zeros_like(acc)

    val = val_ref[...]
    expanded = jnp.dot(val, half[...], preferred_element_type=jnp.float32)
    weighted = (scr_ref[...].astype(jnp.float32) * expanded).astype(jnp.bfloat16)
    acc[...] += lax.dot_general(
        val, weighted, (((0,), (0,)), ((), ())), preferred_element_type=jnp.float32
    )

    @pl.when(step == pl.num_programs(0) - 1)
    def _():
        terms[...] = jnp.dot(
            acc[...].astype(jnp.bfloat16), con_ref[...], preferred_element_type=jnp.float32
        )
        for i, rel_a in enumerate(order_a):
            if i < rows_keep:
                target, rows = keep_refs[i], slice(0, vb)
            else:
                target, rows = send_ref, slice((i - rows_keep) * vb, (i - rows_keep + 1) * vb)
            if aligned:
                for j, rel_b in enumerate(order_b):
                    target[rows, j * cb : (j + 1) * cb] = terms[row(rel_a), column(rel_b)].astype(target.dtype)
            else:
                value = xor_columns(terms[row(rel_a), :], me_b, cb)
                target[rows, :] = jnp.concatenate(
                    [value[:, k * cb : (k + 1) * cb] for k in order_b], axis=1
                ).astype(target.dtype)


def apply_block(me, exc_rows, con, val, screened, order_a, order_b):
    count = len(exc_rows)
    vb, nc = exc_rows[0].shape
    nv = count * vb
    np_, nq = screened.shape
    tile = min(TILE_P, np_)
    keep = max(count // 2, 1)
    whole = lambda shape: pl.BlockSpec(shape, lambda i, m: (0, 0), pipeline_mode=pl.Buffered(1))
    flops = 2 * nv * nc * nq * 2 + 4 * np_ * nq * nv
    *kept, send = pl.pallas_call(
        functools.partial(fused_kernel, order_a, order_b, keep),
        out_shape=[jax.ShapeDtypeStruct((vb, nc), jnp.float32)] * keep
        + [jax.ShapeDtypeStruct((nv - keep * vb, nc), jnp.bfloat16)],
        grid_spec=pltpu.PrefetchScalarGridSpec(
            num_scalar_prefetch=1,
            grid=(np_ // tile,),
            in_specs=[whole((vb, nc))] * count
            + [
                whole((nq, nc)),
                pl.BlockSpec((tile, nv), lambda i, m: (i, 0)),
                pl.BlockSpec((tile, nq), lambda i, m: (i, 0)),
            ],
            out_specs=[whole((vb, nc))] * keep + [whole((nv - keep * vb, nc))],
            scratch_shapes=[
                pltpu.VMEM((nv, nc), jnp.bfloat16),
                pltpu.VMEM((nv, nq), jnp.bfloat16),
                pltpu.VMEM((nv, nq), jnp.float32),
                pltpu.VMEM((nv, nc), jnp.float32),
            ],
        ),
        cost_estimate=pl.CostEstimate(
            flops=flops, transcendentals=0, bytes_accessed=2 * (np_ * nq + np_ * nv + nq * nc)
        ),
    )(me, *exc_rows, con, val, screened)
    return kept, send


def solution(mesh):
    na, nb = mesh.shape["pa"], mesh.shape["pb"]
    low_a, high_a = 2, na // 2
    high_b = min(nb, 4)
    low_b = nb // high_b
    order_a = [h * low_a + l for l in range(low_a) for h in range(high_a)]
    order_b = [h * low_b + l for l in range(low_b) for h in range(high_b)]

    def to_a(x, mask):
        return lax.ppermute(x, "pa", xor_pairs(na, mask))

    def to_b(x, mask):
        return lax.ppermute(x, "pb", xor_pairs(nb, mask))

    def local(excitons, screened, phi_val, phi_con):
        me = jnp.stack([lax.axis_index("pa"), lax.axis_index("pb")]).astype(jnp.int32)
        count = excitons.shape[0]
        vb, cb = excitons.shape[1:]
        f32, bf16 = jnp.float32, jnp.bfloat16
        wide = high_b * cb

        def gather(e):
            own = excitons[e]
            line = jnp.concatenate([own] + [to_b(own, k * low_b) for k in range(1, high_b)], 1)
            row = jnp.concatenate([line] + [to_b(line, k) for k in range(1, low_b)], 1)
            rows = [row] + [to_a(row, k * low_a) for k in range(1, high_a)]
            return rows + [to_a(r, k) for k in range(1, low_a) for r in rows]

        def scatter(kept, send):
            other = to_a(send, 1)
            rows = [k + other[i * vb : (i + 1) * vb].astype(f32) for i, k in enumerate(kept)]
            out = rows[0]
            for k in range(1, high_a):
                out = out + to_a(rows[k].astype(bf16), k * low_a).astype(f32)
            total = out[:, :wide]
            for k in range(1, low_b):
                total = total + to_b(out[:, k * wide : (k + 1) * wide].astype(bf16), k).astype(f32)
            return total

        totals = []
        for e in range(count):
            kept, send = apply_block(me, gather(e), phi_con, phi_val, screened, order_a, order_b)
            totals.append(scatter(kept, send))
        both = jnp.stack(totals)
        result = both[:, :, :cb]
        for k in range(1, high_b):
            result = result + to_b(both[:, :, k * cb : (k + 1) * cb].astype(bf16), k * low_b).astype(f32)
        return result.astype(bf16)

    placed = (P(None, "pa", "pb"), P("pa", "pb"), P("pa", None), P("pb", None))
    return jax.shard_map(
        local, mesh=mesh, in_specs=placed, out_specs=P(None, "pa", "pb"), check_vma=False
    )
```

```python
import functools

import jax
import jax.numpy as jnp
from jax import lax
from jax.experimental import pallas as pl
from jax.experimental.pallas import tpu as pltpu
from jax.sharding import PartitionSpec as P


TILE_P = 512
LANES = 128
VMEM_LIMIT = 44 * 2**20


def xor_pairs(size, mask):
    return [(i, i ^ mask) for i in range(size)]


def xor_columns(value, me, width):
    columns = value.shape[1]
    bit = 1
    while bit * width < columns:
        half = bit * width
        flipped = jnp.concatenate(
            [value[:, (k ^ 1) * half : ((k ^ 1) + 1) * half] for k in range(columns // half)], axis=1
        )
        value = jnp.where(lax.broadcast((me & bit) != 0, value.shape), flipped, value)
        bit *= 2
    return value


def fused_kernel(plan, *refs):
    places_in, places_out, vb, cb, tile = plan
    piece_refs = refs[: len(places_in)]
    con_ref, val_ref, scr_ref = refs[len(places_in) : len(places_in) + 3]
    out_refs = refs[len(places_in) + 3 : len(places_in) + 3 + len(places_out)]
    exc, half, acc, terms, held, sems = refs[len(places_in) + 3 + len(places_out) :]
    me_a, me_b = lax.axis_index("pa"), lax.axis_index("pb")
    aligned = cb % LANES == 0
    slots = held.shape[0]
    tiles = scr_ref.shape[0] // tile

    def fetch(step, slot):
        return pltpu.make_async_copy(
            scr_ref.at[pl.ds(pl.multiple_of(step * tile, tile), tile), :], held.at[slot], sems.at[slot]
        )

    def row(rel):
        return pl.ds(pl.multiple_of((me_a ^ rel) * vb, vb), vb)

    def column(rel):
        return pl.ds(pl.multiple_of((me_b ^ rel) * cb, cb), cb)

    for slot in range(slots):
        fetch(slot, slot).start()

    for ref, (blocks, columns) in zip(piece_refs, places_in):
        for i, rel_a in enumerate(blocks):
            rows = slice(i * vb, (i + 1) * vb)
            if aligned:
                for j, rel_b in enumerate(columns):
                    exc[row(rel_a), column(rel_b)] = ref[rows, j * cb : (j + 1) * cb]
            else:
                value = ref[rows, :]
                value = jnp.concatenate(
                    [value[:, columns.index(k) * cb : (columns.index(k) + 1) * cb] for k in range(len(columns))],
                    axis=1,
                )
                exc[row(rel_a), :] = xor_columns(value, me_b, cb)
    half[...] = lax.dot_general(
        exc[...], con_ref[...], (((1,), (1,)), ((), ())), preferred_element_type=jnp.float32
    ).astype(half.dtype)
    acc[...] = jnp.zeros_like(acc)

    def body(step, carry):
        slot = lax.rem(step, slots)
        fetch(step, slot).wait()
        val = val_ref[pl.ds(pl.multiple_of(step * tile, tile), tile), :]
        expanded = jnp.dot(val, half[...], preferred_element_type=jnp.float32)
        weighted = (held[slot].astype(jnp.float32) * expanded).astype(jnp.bfloat16)

        @pl.when(step + slots < tiles)
        def _():
            fetch(step + slots, slot).start()

        acc[...] += lax.dot_general(
            val, weighted, (((0,), (0,)), ((), ())), preferred_element_type=jnp.float32
        )
        return carry

    lax.fori_loop(0, tiles, body, 0)
    terms[...] = jnp.dot(acc[...].astype(jnp.bfloat16), con_ref[...], preferred_element_type=jnp.float32)
    for ref, places in zip(out_refs, places_out):
        for i, (rel_a, columns) in enumerate(places):
            rows = slice(i * vb, (i + 1) * vb)
            if aligned:
                for j, rel_b in enumerate(columns):
                    ref[rows, j * cb : (j + 1) * cb] = terms[row(rel_a), column(rel_b)].astype(ref.dtype)
            else:
                value = xor_columns(terms[row(rel_a), :], me_b, cb)
                ref[rows, :] = jnp.concatenate(
                    [value[:, k * cb : (k + 1) * cb] for k in columns], axis=1
                ).astype(ref.dtype)


def apply_block(pieces, con, val, screened, places_out, dtypes_out, vb, cb):
    np_, nq = screened.shape
    nv, nc = val.shape[1], con.shape[1]
    tile = min(TILE_P, np_)
    slots = min(3, np_ // tile)
    near = pl.BlockSpec(memory_space=pltpu.VMEM)
    shapes = [(len(p) * vb, len(p[0][1]) * cb) for p in places_out]
    flops = 2 * nv * nc * nq * 2 + 4 * np_ * nq * nv
    plan = (tuple(p[1:] for p in pieces), tuple(places_out), vb, cb, tile)
    return pl.pallas_call(
        functools.partial(fused_kernel, plan),
        out_shape=[jax.ShapeDtypeStruct(s, d) for s, d in zip(shapes, dtypes_out)],
        in_specs=[near] * (len(pieces) + 2) + [pl.BlockSpec(memory_space=pltpu.HBM)],
        out_specs=[near] * len(shapes),
        scratch_shapes=[
            pltpu.VMEM((nv, nc), jnp.bfloat16),
            pltpu.VMEM((nv, nq), jnp.bfloat16),
            pltpu.VMEM((nv, nq), jnp.float32),
            pltpu.VMEM((nv, nc), jnp.float32),
            pltpu.VMEM((slots, tile, nq), jnp.bfloat16),
            pltpu.SemaphoreType.DMA((slots,)),
        ],
        compiler_params=pltpu.CompilerParams(vmem_limit_bytes=VMEM_LIMIT),
        cost_estimate=pl.CostEstimate(
            flops=flops, transcendentals=0, bytes_accessed=2 * (np_ * nq + np_ * nv + nq * nc)
        ),
    )(*[p[0] for p in pieces], con, val, screened)


def bring_kernel(far_ref, near_ref, sem):
    copy = pltpu.make_async_copy(far_ref, near_ref, sem)
    copy.start()
    copy.wait()


def bring_near(array):
    return pl.pallas_call(
        bring_kernel,
        out_shape=pltpu.VMEM(array.shape, array.dtype),
        in_specs=[pl.BlockSpec(memory_space=pltpu.HBM)],
        out_specs=pl.BlockSpec(memory_space=pltpu.VMEM),
        scratch_shapes=[pltpu.SemaphoreType.DMA],
        compiler_params=pltpu.CompilerParams(vmem_limit_bytes=2**20),
    )(array)


def solution(mesh):
    na, nb = mesh.shape["pa"], mesh.shape["pb"]
    low_a, high_a = 2, na // 2
    high_b = min(nb, 4)
    low_b = nb // high_b
    plane = [(a, b) for a in range(high_a) for b in range(low_b)]
    plane = sorted(plane, key=lambda p: -((p[0] != 0) + (p[1] != 0)))
    peers = [p for p in plane if p != (0, 0)]
    line_order = list(range(high_b - 1, 0, -1))

    def to_plane(x, peer):
        a, b = peer[0] * low_a, peer[1]
        if b == 0:
            return lax.ppermute(x, "pa", xor_pairs(na, a))
        if a == 0:
            return lax.ppermute(x, "pb", xor_pairs(nb, b))
        pairs = [(i * nb + j, (i ^ a) * nb + (j ^ b)) for i in range(na) for j in range(nb)]
        return lax.ppermute(x, ("pa", "pb"), pairs)

    def to_core(x, k):
        return lax.ppermute(x, "pa", xor_pairs(na, k))

    def to_line(x, k):
        return lax.ppermute(x, "pb", xor_pairs(nb, k * low_b))

    def local(excitons, screened, phi_val, phi_con):
        count = excitons.shape[0]
        vb, cb = excitons.shape[1:]
        f32, bf16 = jnp.float32, jnp.bfloat16
        wide = high_b * cb
        split = cb % LANES == 0

        def columns(b):
            return tuple(h * low_b + b for h in range(high_b))

        full = sum((columns(b) for b in range(low_b)), ())

        con_near = bring_near(phi_con)
        val_near = bring_near(phi_val)

        arrived = {0: excitons}
        for k in line_order:
            arrived[k] = to_line(excitons, k)
        gathered = []
        for e in range(count):
            line = jnp.concatenate([arrived[k][e] for k in range(high_b)], axis=1)
            early = split and e > 0
            if early:
                line = jnp.concatenate([line] + [to_core(line, c) for c in range(1, low_a)], axis=0)
            got = {(0, 0): line}
            for peer in peers:
                got[peer] = to_plane(line, peer)
            pieces = []
            if early:
                for a, b in plane:
                    blocks = tuple(a * low_a + c for c in range(low_a))
                    pieces.append((got[a, b], blocks, columns(b)))
            else:
                for c in range(low_a):
                    for a in range(high_a):
                        parts = [got[a, b] for b in range(low_b)]
                        if not split:
                            row = jnp.concatenate(parts, axis=1)
                            pieces.append((to_core(row, c) if c else row, (a * low_a + c,), full))
                        else:
                            for b in range(low_b):
                                moved = to_core(parts[b], c) if c else parts[b]
                                pieces.append((moved, (a * low_a + c,), columns(b)))
            gathered.append(pieces)

        sent_places = [
            tuple((a * low_a + c, full) for a in range(high_a)) for c in range(1, low_a)
        ]
        totals = []
        for e in range(count):
            early = split and e < count - 1
            if early:
                places = [tuple((a * low_a + c, columns(b)) for c in range(low_a)) for a, b in plane]
                types = [f32 if p == (0, 0) else bf16 for p in plane]
            elif split:
                places = [((a * low_a, columns(b)),) for a, b in plane] + sent_places
                types = [f32] * len(plane) + [bf16] * len(sent_places)
            else:
                places = [((a * low_a, full),) for a in range(high_a)] + sent_places
                types = [f32] * high_a + [bf16] * len(sent_places)
            outs = apply_block(
                gathered[e], con_near, val_near, screened, places, types, vb, cb
            )
            if early:
                local_sums = dict(zip(plane, outs))
                whole = local_sums[0, 0]
                for peer in peers:
                    whole = whole + to_plane(local_sums[peer], peer).astype(f32)
                own = whole[:vb]
                for c in range(1, low_a):
                    own = own + to_core(whole[c * vb : (c + 1) * vb].astype(bf16), c).astype(f32)
                totals.append(own)
                continue
            kept = outs[: len(outs) - len(sent_places)]
            other = [to_core(x, c + 1).astype(f32) for c, x in enumerate(outs[len(kept) :])]
            total = {}
            for a, b in plane:
                if split:
                    part = kept[plane.index((a, b))]
                else:
                    part = kept[a][:, b * wide : (b + 1) * wide]
                for x in other:
                    part = part + x[a * vb : (a + 1) * vb, b * wide : (b + 1) * wide]
                total[a, b] = part
            whole = total[0, 0]
            for peer in peers:
                whole = whole + to_plane(total[peer].astype(bf16), peer).astype(f32)
            totals.append(whole)
        results = []
        for whole in totals:
            final = whole[:, :cb]
            for k in line_order:
                final = final + to_line(whole[:, k * cb : (k + 1) * cb].astype(bf16), k).astype(f32)
            results.append(final)
        return jnp.stack(results).astype(bf16)

    placed = (P(None, "pa", "pb"), P("pa", "pb"), P("pa", None), P("pb", None))
    return jax.shard_map(local, mesh=mesh, in_specs=placed, out_specs=P(None, "pa", "pb"), check_vma=False)
```

```python
import functools

import jax
import jax.numpy as jnp
from jax import lax
from jax.experimental import pallas as pl
from jax.experimental.pallas import tpu as pltpu
from jax.sharding import PartitionSpec as P


TILE_P = 1024
LANES = 128
VMEM_LIMIT = 44 * 2**20


def xor_pairs(size, mask):
    return [(i, i ^ mask) for i in range(size)]


def xor_columns(value, me, width):
    columns = value.shape[1]
    bit = 1
    while bit * width < columns:
        half = bit * width
        flipped = jnp.concatenate(
            [value[:, (k ^ 1) * half : ((k ^ 1) + 1) * half] for k in range(columns // half)], axis=1
        )
        value = jnp.where(lax.broadcast((me & bit) != 0, value.shape), flipped, value)
        bit *= 2
    return value


def fused_kernel(plan, *refs):
    places_in, places_out, deferred, vb, cb, tile = plan
    piece_refs = refs[: len(places_in)]
    con_ref, val_ref, scr_ref = refs[len(places_in) : len(places_in) + 3]
    given = len(places_in) + 3
    outs = len(places_out) + bool(deferred)
    out_refs = refs[given : given + outs]
    exc, half, acc, terms, held, sems = refs[given + outs :]
    me_a, me_b = lax.axis_index("pa"), lax.axis_index("pb")
    aligned = cb % LANES == 0
    slots = held.shape[0]
    tiles = scr_ref.shape[0] // tile

    def fetch(step, slot):
        return pltpu.make_async_copy(
            scr_ref.at[pl.ds(pl.multiple_of(step * tile, tile), tile), :], held.at[slot], sems.at[slot]
        )

    def row(rel):
        return pl.ds(pl.multiple_of((me_a ^ rel) * vb, vb), vb)

    def column(rel):
        return pl.ds(pl.multiple_of((me_b ^ rel) * cb, cb), cb)

    for slot in range(slots):
        fetch(slot, slot).start()

    for ref, (blocks, columns) in zip(piece_refs, places_in):
        for i, rel_a in enumerate(blocks):
            rows = slice(i * vb, (i + 1) * vb)
            if aligned:
                for j, rel_b in enumerate(columns):
                    exc[row(rel_a), column(rel_b)] = ref[rows, j * cb : (j + 1) * cb]
            else:
                value = ref[rows, :]
                value = jnp.concatenate(
                    [value[:, columns.index(k) * cb : (columns.index(k) + 1) * cb] for k in range(len(columns))],
                    axis=1,
                )
                exc[row(rel_a), :] = xor_columns(value, me_b, cb)
    half[...] = lax.dot_general(
        exc[...], con_ref[...], (((1,), (1,)), ((), ())), preferred_element_type=jnp.float32
    ).astype(half.dtype)
    acc[...] = jnp.zeros_like(acc)

    def body(step, carry):
        slot = lax.rem(step, slots)
        fetch(step, slot).wait()
        val = val_ref[pl.ds(pl.multiple_of(step * tile, tile), tile), :]
        expanded = jnp.dot(val, half[...], preferred_element_type=jnp.float32)
        weighted = (held[slot].astype(jnp.float32) * expanded).astype(jnp.bfloat16)

        @pl.when(step + slots < tiles)
        def _():
            fetch(step + slots, slot).start()

        acc[...] += lax.dot_general(
            val, weighted, (((0,), (0,)), ((), ())), preferred_element_type=jnp.float32
        )
        return carry

    lax.fori_loop(0, tiles, body, 0)
    if deferred:
        send_ref, back_ref = out_refs
        height = len(places_out[0]) * vb
        for i, (rel_a, _) in enumerate(places_out[0]):
            half[i * vb : (i + 1) * vb, :] = acc[row(rel_a), :].astype(half.dtype)
        for i, rel_a in enumerate(deferred):
            back_ref[i * vb : (i + 1) * vb, :] = acc[row(rel_a), :].astype(back_ref.dtype)
        terms[:height, :] = jnp.dot(half[:height, :], con_ref[...], preferred_element_type=jnp.float32)
        for i, (_, columns) in enumerate(places_out[0]):
            rows = slice(i * vb, (i + 1) * vb)
            for j, rel_b in enumerate(columns):
                send_ref[rows, j * cb : (j + 1) * cb] = terms[rows, column(rel_b)].astype(send_ref.dtype)
        return
    terms[...] = jnp.dot(acc[...].astype(jnp.bfloat16), con_ref[...], preferred_element_type=jnp.float32)
    for ref, places in zip(out_refs, places_out):
        for i, (rel_a, columns) in enumerate(places):
            rows = slice(i * vb, (i + 1) * vb)
            if aligned:
                for j, rel_b in enumerate(columns):
                    ref[rows, j * cb : (j + 1) * cb] = terms[row(rel_a), column(rel_b)].astype(ref.dtype)
            else:
                value = xor_columns(terms[row(rel_a), :], me_b, cb)
                ref[rows, :] = jnp.concatenate(
                    [value[:, k * cb : (k + 1) * cb] for k in columns], axis=1
                ).astype(ref.dtype)


def last_kernel(places_out, vb, cb, back_ref, con_ref, *refs):
    out_refs, terms = refs[:-1], refs[-1]
    me_b = lax.axis_index("pb")
    terms[...] = jnp.dot(back_ref[...], con_ref[...], preferred_element_type=jnp.float32)
    for ref, (i, columns) in zip(out_refs, places_out):
        for j, rel_b in enumerate(columns):
            place = pl.ds(pl.multiple_of((me_b ^ rel_b) * cb, cb), cb)
            ref[:, j * cb : (j + 1) * cb] = terms[i * vb : (i + 1) * vb, place]


def apply_last(back, con, places_out, vb, cb):
    rows, nc = back.shape[0], con.shape[1]
    near = pl.BlockSpec(memory_space=pltpu.VMEM)
    return pl.pallas_call(
        functools.partial(last_kernel, places_out, vb, cb),
        out_shape=[jax.ShapeDtypeStruct((vb, len(p[1]) * cb), jnp.float32) for p in places_out],
        in_specs=[near] * 2,
        out_specs=[near] * len(places_out),
        scratch_shapes=[pltpu.VMEM((rows, nc), jnp.float32)],
        compiler_params=pltpu.CompilerParams(vmem_limit_bytes=VMEM_LIMIT),
        cost_estimate=pl.CostEstimate(
            flops=2 * rows * con.shape[0] * nc, transcendentals=0, bytes_accessed=2 * con.size
        ),
    )(back, con)


def apply_block(pieces, con, val, screened, places_out, dtypes_out, vb, cb, deferred=()):
    np_, nq = screened.shape
    nv, nc = val.shape[1], con.shape[1]
    tile = min(TILE_P, np_)
    slots = min(2, np_ // tile)
    near = pl.BlockSpec(memory_space=pltpu.VMEM)
    shapes = [(len(p) * vb, len(p[0][1]) * cb) for p in places_out]
    dtypes_out = list(dtypes_out)
    if deferred:
        shapes.append((len(deferred) * vb, nq))
        dtypes_out.append(jnp.bfloat16)
    flops = 2 * nv * nc * nq * 2 + 4 * np_ * nq * nv
    plan = (tuple(p[1:] for p in pieces), tuple(places_out), tuple(deferred), vb, cb, tile)
    return pl.pallas_call(
        functools.partial(fused_kernel, plan),
        out_shape=[jax.ShapeDtypeStruct(s, d) for s, d in zip(shapes, dtypes_out)],
        in_specs=[near] * (len(pieces) + 2) + [pl.BlockSpec(memory_space=pltpu.HBM)],
        out_specs=[near] * len(shapes),
        scratch_shapes=[
            pltpu.VMEM((nv, nc), jnp.bfloat16),
            pltpu.VMEM((nv, nq), jnp.bfloat16),
            pltpu.VMEM((nv, nq), jnp.float32),
            pltpu.VMEM((nv, nc), jnp.float32),
            pltpu.VMEM((slots, tile, nq), jnp.bfloat16),
            pltpu.SemaphoreType.DMA((slots,)),
        ],
        compiler_params=pltpu.CompilerParams(vmem_limit_bytes=VMEM_LIMIT),
        cost_estimate=pl.CostEstimate(
            flops=flops, transcendentals=0, bytes_accessed=2 * (np_ * nq + np_ * nv + nq * nc)
        ),
    )(*[p[0] for p in pieces], con, val, screened)


def bring_kernel(far_ref, near_ref, sem):
    copy = pltpu.make_async_copy(far_ref, near_ref, sem)
    copy.start()
    copy.wait()


def bring_near(array):
    return pl.pallas_call(
        bring_kernel,
        out_shape=pltpu.VMEM(array.shape, array.dtype),
        in_specs=[pl.BlockSpec(memory_space=pltpu.HBM)],
        out_specs=pl.BlockSpec(memory_space=pltpu.VMEM),
        scratch_shapes=[pltpu.SemaphoreType.DMA],
        compiler_params=pltpu.CompilerParams(vmem_limit_bytes=2**20),
    )(array)


def solution(mesh):
    na, nb = mesh.shape["pa"], mesh.shape["pb"]
    low_a, high_a = 2, na // 2
    high_b = min(nb, 4)
    low_b = nb // high_b
    plane = [(a, b) for a in range(high_a) for b in range(low_b)]
    plane = sorted(plane, key=lambda p: -((p[0] != 0) + (p[1] != 0)))
    peers = [p for p in plane if p != (0, 0)]
    line_order = list(range(high_b - 1, 0, -1))

    def to_plane(x, peer):
        a, b = peer[0] * low_a, peer[1]
        if b == 0:
            return lax.ppermute(x, "pa", xor_pairs(na, a))
        if a == 0:
            return lax.ppermute(x, "pb", xor_pairs(nb, b))
        pairs = [(i * nb + j, (i ^ a) * nb + (j ^ b)) for i in range(na) for j in range(nb)]
        return lax.ppermute(x, ("pa", "pb"), pairs)

    def to_core(x, k):
        return lax.ppermute(x, "pa", xor_pairs(na, k))

    def to_line(x, k):
        return lax.ppermute(x, "pb", xor_pairs(nb, k * low_b))

    def local(excitons, screened, phi_val, phi_con):
        count = excitons.shape[0]
        vb, cb = excitons.shape[1:]
        f32, bf16 = jnp.float32, jnp.bfloat16
        wide = high_b * cb
        split = cb % LANES == 0

        def columns(b):
            return tuple(h * low_b + b for h in range(high_b))

        full = sum((columns(b) for b in range(low_b)), ())

        con_near = bring_near(phi_con)
        val_near = bring_near(phi_val)

        arrived = {0: excitons}
        for k in line_order:
            arrived[k] = to_line(excitons, k)
        gathered = []
        for e in range(count):
            line = jnp.concatenate([arrived[k][e] for k in range(high_b)], axis=1)
            early = split and e > 0
            if early:
                line = jnp.concatenate([line] + [to_core(line, c) for c in range(1, low_a)], axis=0)
            got = {(0, 0): line}
            for peer in peers:
                got[peer] = to_plane(line, peer)
            pieces = []
            if early:
                for a, b in plane:
                    blocks = tuple(a * low_a + c for c in range(low_a))
                    pieces.append((got[a, b], blocks, columns(b)))
            else:
                for c in range(low_a):
                    for a in range(high_a):
                        parts = [got[a, b] for b in range(low_b)]
                        if not split:
                            row = jnp.concatenate(parts, axis=1)
                            pieces.append((to_core(row, c) if c else row, (a * low_a + c,), full))
                        else:
                            for b in range(low_b):
                                moved = to_core(parts[b], c) if c else parts[b]
                                pieces.append((moved, (a * low_a + c,), columns(b)))
            gathered.append(pieces)

        sent_places = [
            tuple((a * low_a + c, full) for a in range(high_a)) for c in range(1, low_a)
        ]
        totals = []
        for e in range(count):
            early = split and e < count - 1
            if early:
                places = [tuple((a * low_a + c, columns(b)) for c in range(low_a)) for a, b in plane]
                types = [f32 if p == (0, 0) else bf16 for p in plane]
            elif split:
                places, types = sent_places, [bf16]
            else:
                places = [((a * low_a, full),) for a in range(high_a)] + sent_places
                types = [f32] * high_a + [bf16] * len(sent_places)
            outs = apply_block(
                gathered[e], con_near, val_near, screened, places, types, vb, cb,
                tuple(a * low_a for a in range(high_a)) if split and not early else (),
            )
            if early:
                local_sums = dict(zip(plane, outs))
                whole = local_sums[0, 0]
                for peer in peers:
                    whole = whole + to_plane(local_sums[peer], peer).astype(f32)
                own = whole[:vb]
                for c in range(1, low_a):
                    own = own + to_core(whole[c * vb : (c + 1) * vb].astype(bf16), c).astype(f32)
                totals.append(own)
                continue
            if split:
                sent, (back,) = outs[:1], outs[1:]
                kept = apply_last(back, con_near, tuple((a, columns(b)) for a, b in plane), vb, cb)
            else:
                kept, sent = outs[:high_a], outs[high_a:]
            other = [to_core(x, c + 1).astype(f32) for c, x in enumerate(sent)]
            total = {}
            for a, b in plane:
                if split:
                    part = kept[plane.index((a, b))]
                else:
                    part = kept[a][:, b * wide : (b + 1) * wide]
                for x in other:
                    part = part + x[a * vb : (a + 1) * vb, b * wide : (b + 1) * wide]
                total[a, b] = part
            whole = total[0, 0]
            for peer in peers:
                whole = whole + to_plane(total[peer].astype(bf16), peer).astype(f32)
            totals.append(whole)
        results = []
        for whole in totals:
            final = whole[:, :cb]
            for k in line_order:
                final = final + to_line(whole[:, k * cb : (k + 1) * cb].astype(bf16), k).astype(f32)
            results.append(final)
        return jnp.stack(results).astype(bf16)

    placed = (P(None, "pa", "pb"), P("pa", "pb"), P("pa", None), P("pb", None))
    return jax.shard_map(local, mesh=mesh, in_specs=placed, out_specs=P(None, "pa", "pb"), check_vma=False)
```
